32 devices in a mesh: mem: 8 (over z, y), job: 4 (over x, core).
Axes of the slice: x: 2, y: 2, z: 4, core: 2. Of those that a mesh axis runs over, the one named last changes fastest.
Arguments:
- pair_cost: bfloat16 [1536, 128, 128], P(('mem', 'job')), may hold values from -6 to 6
- pair_coef: bfloat16 [1536, 128, 128], P(('mem', 'job')), may hold values from 0.049804688 to 0.5
- slot_member: int32 [32, 48], P(('mem', 'job')), may hold values from 0 to 31, never falling along the last dimension, each value on 1 to 4 neighbouring positions
- slot_owner: int32 [32, 48, 1], P(('mem', 'job')), may hold values from 0 to 7; in each aligned block of 48 rows (0 to 47, 48 to 95, ..., all dimensions but the last counted through in order) at most 9 rows name the same one
- slot_local: int32 [32, 48], P(('mem', 'job')), may hold values from 0 to 15
- duals: float32 [512, 128], P(('mem', 'job')), may hold values from 0.1 to 3
- capacity: int32 [512, 128], P(('mem', 'job')), may hold values from 0 to 39
Outputs:
- primal: bfloat16 [1536, 128, 128], P(('mem', 'job'))
- gradient: float32 [512, 128], P(('mem', 'job'))
- member_share: float32 [256, 128], P('mem')
The draws below stay inside these ranges and needn't reach their ends.
Inputs may be any that keep to these rules, and one draw needn't show every extreme that they name: `slot_member`: in each device's row the values never fall, every value appears, none more than 4 times, and one exactly 4 times. `slot_owner`: among the 48 entries of one device no value appears more than 9 times, and in some devices one appears exactly 9 times.
All inputs are finite; a program needn't handle non-finite values.
Results may differ from the reference program's by a relative error of at most 0.001.
Values sent between devices are 32-bit elements; how exact they have to be, the bound alone decides.
A program may use at most 64 MiB of HBM per device.

```python
import math
import jax
import jax.numpy as jnp
import numpy as np
from jax import lax

BLOCK = 128
CAP = 48
MB_DEV = 32
JB_DEV = 16
SEG_MOST = 4
PEER_MOST = 9
NBLK = 1536
MBLK = 256
JBLK = 512
N_MEM = 8
N_JOB = 4


def plant(array, key, least, high):
    place = [jax.random.randint(jax.random.fold_in(key, axis), (), 0, length) for axis, length in enumerate(array.shape)]
    longest = array.shape.index(max(array.shape))
    neighbour = place[:longest] + [(place[longest] + 1) % array.shape[longest]] + place[longest + 1:]
    return array.at[tuple(place)].set(least).at[tuple(neighbour)].set(high)


def shard_levels(key, shape, pieces, least, high):
    def one(position, blocks):
        draws = jax.random.uniform(jax.random.fold_in(jax.random.fold_in(key, 6), position), (blocks,), jnp.float32, least / len(pieces), high / len(pieces))
        return jnp.repeat(jnp.exp(draws), shape[position] // blocks).reshape((-1,) + (1,) * (len(shape) - position - 1))

    factor_of = one(*pieces[0])
    for cut in pieces[1:]:
        factor_of = factor_of * one(*cut)
    return factor_of


def split_up(number_of, total, reach, lean):
    portions = [(1 << 20) // math.isqrt(grade ** lean) + 1 for grade in range(2, number_of + 1)]
    rest, counts = total - reach - (number_of - 1), [1] * (number_of - 1)
    while rest > 0:
        candidates = [i for i in range(number_of - 1) if counts[i] < reach]
        mass, left = sum([portions[i] for i in candidates]), rest
        for i in candidates:
            more = min(reach - counts[i], max(1, left * portions[i] // mass), rest)
            counts[i] = counts[i] + more
            rest = rest - more
    return np.array([reach] + counts)


def uneven(rng, amount, total, limit, slope):
    if amount == 2:
        one = jax.random.randint(rng, (), max(1, total - limit), min(limit, total - 1) + 1)
        return jnp.stack([one, total - one])
    sizes = jnp.asarray(split_up(amount, total, limit, slope), jnp.int32)
    couples = (amount - 1) // 2
    source_of, receiver = sizes[1:1 + 2 * couples:2], sizes[2:2 + 2 * couples:2]
    slack = jnp.minimum(source_of - 1, limit - receiver)
    passed = jax.random.randint(jax.random.fold_in(rng, 1), (couples,), 0, 1 << 20) % (slack + 1)
    sizes = sizes.at[1:1 + 2 * couples:2].set(source_of - passed).at[2:2 + 2 * couples:2].set(receiver + passed)
    return sizes[jax.random.permutation(jax.random.fold_in(rng, 2), amount)]


def shared_out(own_key, own, number, rows, amount, top, limit, skew):
    ranking = jax.random.permutation(own_key, amount)
    crowded, ordinary = shares(amount, rows * top, limit, skew, True), shares(amount, rows * top, limit, skew, False)
    places = jnp.arange(amount)

    def named(sizes, offset_by):
        used = int((sizes > 0).sum())
        fixed = max(1, used // 4)
        moved = fixed + (places - fixed + offset_by * (used - fixed)) % max(1, amount - fixed)
        return jnp.zeros((amount,), jnp.int32).at[ranking[jnp.where(places < fixed, places, moved)]].set(jnp.asarray(sizes, jnp.int32))

    sizes = jnp.where(number % 4 == 0, named(crowded, number // 4), named(ordinary, number - number // 4 - 1))
    mixed = jax.random.permutation(jax.random.fold_in(own, 3), amount)
    giver, receiver = mixed[0:amount // 2 * 2:2], mixed[1:amount // 2 * 2:2]
    room = jnp.minimum(sizes[giver] - 1, limit - sizes[receiver]) // 2
    room = jnp.where((giver == ranking[0]) | (receiver == ranking[0]) | (sizes[receiver] == 0), 0, jnp.maximum(room, 0))
    moved = jax.random.randint(jax.random.fold_in(own, 4), (amount // 2,), 0, 1 << 20) % (room + 1)
    sizes = sizes.at[giver].add(-moved).at[receiver].add(moved)
    items = jnp.searchsorted(jnp.cumsum(sizes), jnp.arange(rows * top), side="right").astype(jnp.int32)
    grid = items.reshape(top, rows).T
    grid = grid[jax.random.permutation(jax.random.fold_in(own, 1), rows)]
    offset_by = jax.random.randint(jax.random.fold_in(own, 2), (rows, 1), 0, top)
    return jnp.take_along_axis(grid, (jnp.arange(top)[None, :] + offset_by) % top, axis=1)


def shares(number_of, total, reach, skew, full):
    weights = [(1 << 20) // math.isqrt(standing ** skew) + 1 for standing in range(1, number_of + 1)]
    largest = reach if full else min(reach, max(-(-total // number_of), total * weights[0] // sum(weights)))
    least = 1 if total - largest >= number_of - 1 else 0
    holding, rest = [largest] + [least] * (number_of - 1), total - largest - least * (number_of - 1)
    while rest > 0:
        candidates = [i for i in range(1, number_of) if holding[i] < largest] or [i for i in range(1, number_of) if holding[i] < reach]
        mass, budget = sum([weights[i] for i in candidates]), rest
        for i in candidates:
            addition = min(reach - holding[i], max(1, budget * weights[i] // mass), rest)
            holding[i] = holding[i] + addition
            rest = rest - addition
    return np.array(holding)


def gaussian(key, extent, width, bound, shards=(), kind=jnp.bfloat16):
    level = shard_levels(key, extent, shards, -0.22, 0.18) if shards else 1.0
    array = jax.random.normal(key, extent, jnp.float32) * width * level
    return jnp.minimum(jnp.maximum(array, -bound), bound).astype(kind)


def setup_inputs(seed: int = 0) -> dict:
    keys = jax.random.split(jax.random.key(seed), 8)
    pair_cost = gaussian(keys[0], (NBLK, BLOCK, BLOCK), 1.0, 6.0, ((0, 32),))
    pair_coef = jnp.clip(jnp.exp(math.log(0.5) - 2.306499 * jax.random.uniform(keys[1], (NBLK, BLOCK, BLOCK), jnp.float32) ** shard_levels(keys[1], (NBLK, BLOCK, BLOCK), ((0, 32),), -0.2, 0.2)), 0.049804688, 0.5).astype(jnp.bfloat16)
    slot_member = jax.vmap(lambda own: jnp.searchsorted(jnp.cumsum(uneven(own, MB_DEV, CAP, SEG_MOST, 2)), jnp.arange(CAP), side="right"))(jax.random.split(keys[2], (N_MEM * N_JOB))).reshape((N_MEM * N_JOB, CAP)).astype(jnp.int32)
    slot_owner_keys = jax.random.split(jax.random.fold_in(keys[3], 1), (N_MEM * N_JOB) * CAP // CAP)
    slot_owner_turns = jax.random.permutation(jax.random.fold_in(keys[3], 3), (N_MEM * N_JOB) * CAP // CAP)
    slot_owner = jax.vmap(lambda own, number: shared_out(jax.random.fold_in(keys[3], 2), own, number, CAP, N_MEM, 1, PEER_MOST, 2))(slot_owner_keys, slot_owner_turns).reshape((N_MEM * N_JOB, CAP, 1))
    slot_local = plant(jax.random.randint(keys[4], (N_MEM * N_JOB, CAP), 0, JB_DEV), jax.random.fold_in(keys[4], 1), 0, JB_DEV - 1).astype(jnp.int32)
    duals = jnp.clip(jnp.exp(math.log(3.0) - 3.4011974 * jax.random.uniform(keys[5], (JBLK, BLOCK), jnp.float32) ** shard_levels(keys[5], (JBLK, BLOCK), ((0, 32),), -0.2, 0.2)), 0.1, 3.0)
    capacity = plant(jax.random.randint(keys[6], (JBLK, BLOCK), 0, 40), jax.random.fold_in(keys[6], 1), 0, 39).astype(jnp.int32)
    return dict(pair_cost=pair_cost, pair_coef=pair_coef, slot_member=slot_member, slot_owner=slot_owner, slot_local=slot_local, duals=duals, capacity=capacity)


RIDGE = 1.0


def slot_terms(packed):
    pair_cost, pair_coef, dual_rows = packed
    reduced = pair_cost.astype(jnp.float32) + pair_coef.astype(jnp.float32) * dual_rows[:, None, :]
    allocation = jnp.clip(-reduced / RIDGE, 0.0, 1.0)
    column_part = jnp.sum(pair_coef.astype(jnp.float32) * allocation, axis=1)
    row_part = jnp.sum(allocation, axis=2)
    return allocation.astype(jnp.bfloat16), column_part, row_part


def reference(pair_cost, pair_coef, slot_member, slot_owner, slot_local, duals, capacity):
    device = jnp.arange(N_MEM * N_JOB, dtype=jnp.int32)
    column = device % N_JOB
    job_block = (slot_owner[:, :, 0] * N_JOB + column[:, None]) * JB_DEV + slot_local
    member_block = (device // N_JOB)[:, None] * MB_DEV + slot_member
    dual_rows = duals[job_block.reshape(-1)].reshape(N_MEM * N_JOB, CAP, BLOCK)
    cost_dev = pair_cost.reshape(N_MEM * N_JOB, CAP, BLOCK, BLOCK)
    coef_dev = pair_coef.reshape(N_MEM * N_JOB, CAP, BLOCK, BLOCK)
    primal, column_part, row_part = lax.map(slot_terms, (cost_dev, coef_dev, dual_rows))
    totals = jax.ops.segment_sum(column_part.reshape(-1, BLOCK), job_block.reshape(-1).astype(jnp.int32), num_segments=JBLK)
    gradient = totals - capacity.astype(jnp.float32)
    members = jax.ops.segment_sum(row_part.reshape(-1, BLOCK), member_block.reshape(-1).astype(jnp.int32), num_segments=MBLK)
    member_share = members / BLOCK
    return primal.reshape(NBLK, BLOCK, BLOCK), gradient, member_share
```

```python
import functools

import jax
import jax.numpy as jnp
from jax import lax
from jax.experimental import pallas as pl
from jax.experimental.pallas import tpu as pltpu
from jax.sharding import PartitionSpec as P

MB_DEV = 32
CHUNK = 8

MESH = pl.DeviceIdType.MESH


def kernel(
    mem_count,
    job_count,
    cost_ref,
    coef_ref,
    member_ref,
    owner_ref,
    local_ref,
    duals_ref,
    capacity_ref,
    primal_ref,
    gradient_ref,
    share_ref,
    cost_v,
    coef_v,
    primal_v,
    member_s,
    owner_s,
    local_s,
    owner_v,
    local_v,
    capacity_v,
    table,
    column,
    totals,
    incoming,
    member_part,
    member_in,
    load_sem,
    small_sem,
    store_sem,
    gather_send,
    gather_recv,
    column_send,
    column_recv,
    member_send,
    member_recv,
):
    slots, block = cost_v.shape[0], cost_v.shape[1]
    jobs = duals_ref.shape[0]
    chunk = min(CHUNK, slots)
    chunks = slots // chunk
    my_mem = lax.axis_index("mem")
    my_job = lax.axis_index("job")

    barrier = pltpu.get_barrier_semaphore()

    def mem_peer(step):
        return lax.rem(my_mem + step, mem_count)

    def job_peer(step):
        return lax.rem(my_job + step, job_count)

    for step in range(1, mem_count):
        pl.semaphore_signal(
            barrier, inc=1, device_id=(mem_peer(step), my_job), device_id_type=MESH
        )
    for step in range(1, job_count):
        pl.semaphore_signal(
            barrier, inc=1, device_id=(my_mem, job_peer(step)), device_id_type=MESH
        )

    own_rows = pl.ds(pl.multiple_of(my_mem * jobs, jobs), jobs)
    small = [
        pltpu.make_async_copy(duals_ref, table.at[own_rows], small_sem.at[0]),
        pltpu.make_async_copy(owner_ref, owner_s, small_sem.at[1]),
        pltpu.make_async_copy(local_ref, local_s, small_sem.at[2]),
        pltpu.make_async_copy(member_ref, member_s, small_sem.at[3]),
        pltpu.make_async_copy(owner_ref, owner_v, small_sem.at[4]),
        pltpu.make_async_copy(local_ref, local_v, small_sem.at[5]),
        pltpu.make_async_copy(capacity_ref, capacity_v, small_sem.at[6]),
    ]
    for copy in small:
        copy.start()
    loads = []
    for part in range(chunks):
        rows = pl.ds(part * chunk, chunk)
        for index, (source, target) in enumerate(((cost_ref, cost_v), (coef_ref, coef_v))):
            copy = pltpu.make_async_copy(
                source.at[rows], target.at[rows], load_sem.at[2 * part + index]
            )
            copy.start()
            loads.append(copy)
    small[0].wait()

    pl.semaphore_wait(barrier, mem_count + job_count - 2)

    gathers = []
    for step in range(1, mem_count):
        copy = pltpu.make_async_remote_copy(
            src_ref=table.at[own_rows],
            dst_ref=table.at[own_rows],
            send_sem=gather_send.at[step - 1],
            recv_sem=gather_recv.at[step - 1],
            device_id=(mem_peer(step), my_job),
            device_id_type=MESH,
        )
        copy.start()
        gathers.append(copy)
    for copy in small[1:]:
        copy.wait()
    for copy in loads:
        copy.wait()
    for copy in gathers:
        copy.wait_recv()

    lanes = lax.broadcasted_iota(jnp.int32, (block, block), 1)
    stores = []
    members = jnp.zeros((block, block), jnp.float32)
    for part in range(chunks):

        def pair(index, members, part=part):
            halves = []
            marks = []
            for side in range(2):
                slot = part * chunk + 2 * index + side
                row = owner_s[0, slot] * jobs + local_s[0, slot]
                dual = -table[pl.ds(row, 1), :]
                coef = coef_v[slot].astype(jnp.float32)
                allocation = jnp.clip(
                    coef * dual - cost_v[slot].astype(jnp.float32), 0.0, 1.0
                )
                primal = allocation.astype(jnp.bfloat16)
                primal_v[slot] = primal
                column[pl.ds(slot, 1), :] = jnp.sum(coef * allocation, axis=0, keepdims=True)
                halves.append(primal)
                marks.append((lanes == member_s[0, slot]).astype(jnp.float32).astype(jnp.bfloat16))
            return members + jnp.dot(
                jnp.concatenate(halves, axis=1),
                jnp.concatenate(marks, axis=0),
                preferred_element_type=jnp.float32,
            )

        members = lax.fori_loop(0, chunk // 2, pair, members, unroll=2)
        rows = pl.ds(part * chunk, chunk)
        copy = pltpu.make_async_copy(primal_v.at[rows], primal_ref.at[rows], store_sem.at[part])
        copy.start()
        stores.append(copy)

    named = owner_v[...] * jobs + local_v[...]
    match = lax.broadcasted_iota(jnp.int32, (mem_count * jobs, slots), 0) == named
    match = match.astype(jnp.float32).astype(jnp.bfloat16)
    sums = column[...]
    high = sums.astype(jnp.bfloat16)
    low = (sums - high.astype(jnp.float32)).astype(jnp.bfloat16)
    totals[...] = jnp.dot(match, high, preferred_element_type=jnp.float32) + jnp.dot(
        match, low, preferred_element_type=jnp.float32
    )
    member_part[...] = members.T[:MB_DEV]

    sends = []
    for step in range(1, mem_count):
        peer = mem_peer(step)
        copy = pltpu.make_async_remote_copy(
            src_ref=totals.at[pl.ds(pl.multiple_of(peer * jobs, jobs), jobs)],
            dst_ref=incoming.at[step - 1],
            send_sem=column_send.at[step - 1],
            recv_sem=column_recv.at[step - 1],
            device_id=(peer, my_job),
            device_id_type=MESH,
        )
        copy.start()
        sends.append(copy)
    shares = []
    for step in range(1, job_count):
        copy = pltpu.make_async_remote_copy(
            src_ref=member_part,
            dst_ref=member_in.at[step - 1],
            send_sem=member_send.at[step - 1],
            recv_sem=member_recv.at[step - 1],
            device_id=(my_mem, job_peer(step)),
            device_id_type=MESH,
        )
        copy.start()
        shares.append(copy)

    share = member_part[...]
    for step, copy in enumerate(shares):
        copy.wait_recv()
        share = share + member_in[step]
    share_ref[...] = share * (1.0 / block)

    gradient = totals[own_rows, :] - capacity_v[...].astype(jnp.float32)
    for step, copy in enumerate(sends):
        copy.wait_recv()
        gradient = gradient + incoming[step]
    gradient_ref[...] = gradient

    for copy in gathers + sends + shares:
        copy.wait_send()
    for copy in stores:
        copy.wait()


def solution(mesh):
    mem_count, job_count = mesh.shape["mem"], mesh.shape["job"]
    row = P(("mem", "job"))

    def per_device(pair_cost, pair_coef, slot_member, slot_owner, slot_local, duals, capacity):
        slots, block, _ = pair_cost.shape
        jobs = duals.shape[0]
        chunks = slots // min(CHUNK, slots)
        anywhere = pl.BlockSpec(memory_space=pl.ANY)
        dma = pltpu.SemaphoreType.DMA
        return pl.pallas_call(
            functools.partial(kernel, mem_count, job_count),
            out_shape=(
                jax.ShapeDtypeStruct(pair_cost.shape, jnp.bfloat16),
                jax.ShapeDtypeStruct((jobs, block), jnp.float32),
                jax.ShapeDtypeStruct((MB_DEV, block), jnp.float32),
            ),
            in_specs=[anywhere] * 7,
            out_specs=(
                anywhere,
                pl.BlockSpec(memory_space=pltpu.VMEM),
                pl.BlockSpec(memory_space=pltpu.VMEM),
            ),
            scratch_shapes=[
                pltpu.VMEM(pair_cost.shape, jnp.bfloat16),
                pltpu.VMEM(pair_cost.shape, jnp.bfloat16),
                pltpu.VMEM(pair_cost.shape, jnp.bfloat16),
                pltpu.SMEM((1, slots), jnp.int32),
                pltpu.SMEM((1, slots), jnp.int32),
                pltpu.SMEM((1, slots), jnp.int32),
                pltpu.VMEM((1, slots), jnp.int32),
                pltpu.VMEM((1, slots), jnp.int32),
                pltpu.VMEM((jobs, block), jnp.int32),
                pltpu.VMEM((mem_count * jobs, block), jnp.float32),
                pltpu.VMEM((slots, block), jnp.float32),
                pltpu.VMEM((mem_count * jobs, block), jnp.float32),
                pltpu.VMEM((mem_count - 1, jobs, block), jnp.float32),
                pltpu.VMEM((MB_DEV, block), jnp.float32),
                pltpu.VMEM((job_count - 1, MB_DEV, block), jnp.float32),
                dma((2 * chunks,)),
                dma((7,)),
                dma((chunks,)),
                dma((mem_count - 1,)),
                dma((mem_count - 1,)),
                dma((mem_count - 1,)),
                dma((mem_count - 1,)),
                dma((job_count - 1,)),
                dma((job_count - 1,)),
            ],
            compiler_params=pltpu.CompilerParams(collective_id=0, has_side_effects=True),
        )(
            pair_cost,
            pair_coef,
            slot_member,
            slot_owner.reshape(1, slots),
            slot_local,
            duals,
            capacity,
        )

    return jax.shard_map(
        per_device,
        mesh=mesh,
        in_specs=(row,) * 7,
        out_specs=(row, row, P("mem")),
        check_vma=False,
    )
```

```python
import functools

import jax
import jax.numpy as jnp
from jax import lax
from jax.experimental import pallas as pl
from jax.experimental.pallas import tpu as pltpu
from jax.sharding import PartitionSpec as P

MB_DEV = 32
CHUNK = 8
VMEM_LIMIT = 16 << 20

MESH = pl.DeviceIdType.MESH


def partner(index, distance, count):
    assert count & (count - 1) == 0
    bit = 1
    while bit < count:
        if distance & bit:
            index = index + bit - 2 * bit * ((index // bit) % 2)
        bit *= 2
    return index


def finish(primal_in, gradient_in, share_in, primal_ref, gradient_ref, share_ref, sem):
    copies = [
        pltpu.make_async_copy(primal_in, primal_ref, sem.at[0]),
        pltpu.make_async_copy(gradient_in, gradient_ref, sem.at[1]),
        pltpu.make_async_copy(share_in, share_ref, sem.at[2]),
    ]
    for copy in copies:
        copy.start()
    for copy in copies:
        copy.wait()


def kernel(
    mem_count,
    job_count,
    cost_ref,
    coef_ref,
    member_ref,
    owner_ref,
    local_ref,
    duals_ref,
    capacity_ref,
    primal_ref,
    gradient_ref,
    share_ref,
    cost_v,
    coef_v,
    member_s,
    owner_s,
    local_s,
    owner_v,
    local_v,
    capacity_v,
    table,
    column,
    totals,
    incoming,
    member_part,
    member_in,
    load_sem,
    small_sem,
    gather_send,
    gather_recv,
    column_send,
    column_recv,
    member_send,
    member_recv,
):
    slots, block = cost_v.shape[0], cost_v.shape[1]
    jobs = duals_ref.shape[0]
    chunk = min(CHUNK, slots)
    chunks = slots // chunk
    my_mem = lax.axis_index("mem")
    my_job = lax.axis_index("job")

    barrier = pltpu.get_barrier_semaphore()

    def mem_peer(step):
        return partner(my_mem, mem_count - step, mem_count)

    def job_peer(step):
        return partner(my_job, job_count - step, job_count)

    for step in range(1, mem_count):
        pl.semaphore_signal(
            barrier, inc=1, device_id=(mem_peer(step), my_job), device_id_type=MESH
        )
    for step in range(1, job_count):
        pl.semaphore_signal(
            barrier, inc=1, device_id=(my_mem, job_peer(step)), device_id_type=MESH
        )

    own_rows = pl.ds(pl.multiple_of(my_mem * jobs, jobs), jobs)
    small = [
        pltpu.make_async_copy(duals_ref, table.at[own_rows], small_sem.at[0]),
        pltpu.make_async_copy(owner_ref, owner_s, small_sem.at[1]),
        pltpu.make_async_copy(local_ref, local_s, small_sem.at[2]),
        pltpu.make_async_copy(member_ref, member_s, small_sem.at[3]),
        pltpu.make_async_copy(owner_ref, owner_v, small_sem.at[4]),
        pltpu.make_async_copy(local_ref, local_v, small_sem.at[5]),
        pltpu.make_async_copy(capacity_ref, capacity_v, small_sem.at[6]),
    ]
    for copy in small:
        copy.start()
    loads = []
    for part in range(chunks):
        rows = pl.ds(part * chunk, chunk)
        for index, (source, target) in enumerate(((cost_ref, cost_v), (coef_ref, coef_v))):
            copy = pltpu.make_async_copy(
                source.at[rows], target.at[rows], load_sem.at[2 * part + index]
            )
            copy.start()
            loads.append(copy)
    small[0].wait()

    pl.semaphore_wait(barrier, mem_count + job_count - 2)

    gathers = []
    for step in range(1, mem_count):
        copy = pltpu.make_async_remote_copy(
            src_ref=table.at[own_rows],
            dst_ref=table.at[own_rows],
            send_sem=gather_send.at[step - 1],
            recv_sem=gather_recv.at[step - 1],
            device_id=(mem_peer(step), my_job),
            device_id_type=MESH,
        )
        copy.start()
        gathers.append(copy)
    for copy in small[1:]:
        copy.wait()
    for copy in loads:
        copy.wait()
    for copy in gathers:
        copy.wait_recv()

    lanes = lax.broadcasted_iota(jnp.int32, (block, block), 1)
    members = jnp.zeros((block, block), jnp.float32)
    for part in range(chunks):

        def pair(index, members, part=part):
            halves = []
            marks = []
            for side in range(2):
                slot = part * chunk + 2 * index + side
                row = owner_s[0, slot] * jobs + local_s[0, slot]
                dual = -table[pl.ds(row, 1), :]
                coef = coef_v[slot].astype(jnp.float32)
                allocation = jnp.clip(
                    coef * dual - cost_v[slot].astype(jnp.float32), 0.0, 1.0
                )
                primal = allocation.astype(jnp.bfloat16)
                primal_ref[slot] = primal
                column[pl.ds(slot, 1), :] = jnp.sum(coef * allocation, axis=0, keepdims=True)
                halves.append(primal)
                marks.append((lanes == member_s[0, slot]).astype(jnp.float32).astype(jnp.bfloat16))
            return members + jnp.dot(
                jnp.concatenate(halves, axis=1),
                jnp.concatenate(marks, axis=0),
                preferred_element_type=jnp.float32,
            )

        members = lax.fori_loop(0, chunk // 2, pair, members, unroll=2)

    named = owner_v[...] * jobs + local_v[...]
    match = lax.broadcasted_iota(jnp.int32, (mem_count * jobs, slots), 0) == named
    match = match.astype(jnp.float32).astype(jnp.bfloat16)
    sums = column[...]
    high = sums.astype(jnp.bfloat16)
    low = (sums - high.astype(jnp.float32)).astype(jnp.bfloat16)
    totals[...] = jnp.dot(match, high, preferred_element_type=jnp.float32) + jnp.dot(
        match, low, preferred_element_type=jnp.float32
    )
    member_part[...] = members.T[:MB_DEV]

    sends = []
    for step in range(1, mem_count):
        peer = mem_peer(step)
        copy = pltpu.make_async_remote_copy(
            src_ref=totals.at[pl.ds(pl.multiple_of(peer * jobs, jobs), jobs)],
            dst_ref=incoming.at[step - 1],
            send_sem=column_send.at[step - 1],
            recv_sem=column_recv.at[step - 1],
            device_id=(peer, my_job),
            device_id_type=MESH,
        )
        copy.start()
        sends.append(copy)
    shares = []
    for step in range(1, job_count):
        copy = pltpu.make_async_remote_copy(
            src_ref=member_part,
            dst_ref=member_in.at[step - 1],
            send_sem=member_send.at[step - 1],
            recv_sem=member_recv.at[step - 1],
            device_id=(my_mem, job_peer(step)),
            device_id_type=MESH,
        )
        copy.start()
        shares.append(copy)

    share = member_part[...]
    for step, copy in enumerate(shares):
        copy.wait_recv()
        share = share + member_in[step]
    share_ref[...] = share * (1.0 / block)

    gradient = totals[own_rows, :] - capacity_v[...].astype(jnp.float32)
    for step, copy in enumerate(sends):
        copy.wait_recv()
        gradient = gradient + incoming[step]
    gradient_ref[...] = gradient

    for copy in gathers + sends + shares:
        copy.wait_send()


def solution(mesh):
    mem_count, job_count = mesh.shape["mem"], mesh.shape["job"]
    row = P(("mem", "job"))

    def per_device(pair_cost, pair_coef, slot_member, slot_owner, slot_local, duals, capacity):
        slots, block, _ = pair_cost.shape
        jobs = duals.shape[0]
        chunks = slots // min(CHUNK, slots)
        hbm = pl.BlockSpec(memory_space=pltpu.HBM)
        vmem = pl.BlockSpec(memory_space=pltpu.VMEM)
        dma = pltpu.SemaphoreType.DMA
        out_shape = (
            jax.ShapeDtypeStruct(pair_cost.shape, jnp.bfloat16),
            jax.ShapeDtypeStruct((jobs, block), jnp.float32),
            jax.ShapeDtypeStruct((MB_DEV, block), jnp.float32),
        )
        operands = (
            pair_cost,
            pair_coef,
            slot_member,
            slot_owner.reshape(1, slots),
            slot_local,
            duals,
            capacity,
        )
        operands = [pltpu.with_memory_space_constraint(value, pltpu.HBM) for value in operands]
        results = pl.pallas_call(
            functools.partial(kernel, mem_count, job_count),
            out_shape=out_shape,
            in_specs=[hbm] * 7,
            out_specs=(vmem,) * 3,
            scratch_shapes=[
                pltpu.VMEM(pair_cost.shape, jnp.bfloat16),
                pltpu.VMEM(pair_cost.shape, jnp.bfloat16),
                pltpu.SMEM((1, slots), jnp.int32),
                pltpu.SMEM((1, slots), jnp.int32),
                pltpu.SMEM((1, slots), jnp.int32),
                pltpu.VMEM((1, slots), jnp.int32),
                pltpu.VMEM((1, slots), jnp.int32),
                pltpu.VMEM((jobs, block), jnp.int32),
                pltpu.VMEM((mem_count * jobs, block), jnp.float32),
                pltpu.VMEM((slots, block), jnp.float32),
                pltpu.VMEM((mem_count * jobs, block), jnp.float32),
                pltpu.VMEM((mem_count - 1, jobs, block), jnp.float32),
                pltpu.VMEM((MB_DEV, block), jnp.float32),
                pltpu.VMEM((job_count - 1, MB_DEV, block), jnp.float32),
                dma((2 * chunks,)),
                dma((7,)),
                dma((mem_count - 1,)),
                dma((mem_count - 1,)),
                dma((mem_count - 1,)),
                dma((mem_count - 1,)),
                dma((job_count - 1,)),
                dma((job_count - 1,)),
            ],
            compiler_params=pltpu.CompilerParams(collective_id=0, has_side_effects=True, vmem_limit_bytes=VMEM_LIMIT),
)(*operands)
        return pl.pallas_call(
            finish,
            out_shape=out_shape,
            in_specs=[pl.BlockSpec(memory_space=pl.ANY)] * 3,
            out_specs=(hbm,) * 3,
            scratch_shapes=[dma((3,))],
            compiler_params=pltpu.CompilerParams(vmem_limit_bytes=VMEM_LIMIT),
        )(*results)

    return jax.shard_map(
        per_device,
        mesh=mesh,
        in_specs=(row,) * 7,
        out_specs=(row, row, P("mem")),
        check_vma=False,
    )
```

```python
import functools

import jax
import jax.numpy as jnp
from jax import lax
from jax.experimental import pallas as pl
from jax.experimental.pallas import tpu as pltpu
from jax.sharding import PartitionSpec as P

MB_DEV = 32
CHUNK = 8
LEVELS = 4
VMEM_LIMIT = 16 << 20

MESH = pl.DeviceIdType.MESH


def partner(index, distance, count):
    assert count & (count - 1) == 0
    bit = 1
    while bit < count:
        if distance & bit:
            index = index + bit - 2 * bit * ((index // bit) % 2)
        bit *= 2
    return index


def finish(primal_in, gradient_in, share_in, primal_ref, gradient_ref, share_ref, sem):
    copies = [
        pltpu.make_async_copy(primal_in, primal_ref, sem.at[0]),
        pltpu.make_async_copy(gradient_in, gradient_ref, sem.at[1]),
        pltpu.make_async_copy(share_in, share_ref, sem.at[2]),
    ]
    for copy in copies:
        copy.start()
    for copy in copies:
        copy.wait()


def kernel(
    mem_count,
    job_count,
    low,
    cost_ref,
    coef_ref,
    member_ref,
    owner_ref,
    local_ref,
    duals_ref,
    capacity_ref,
    primal_ref,
    gradient_ref,
    share_ref,
    cost_v,
    coef_v,
    member_s,
    owner_s,
    local_s,
    owner_v,
    local_v,
    capacity_v,
    table,
    column,
    totals,
    incoming,
    member_part,
    member_in,
    load_sem,
    small_sem,
    beside_send,
    beside_recv,
    down_send,
    down_recv,
    up_send,
    up_recv,
    column_send,
    column_recv,
    member_send,
    member_recv,
):
    slots, block = cost_v.shape[0], cost_v.shape[1]
    jobs = duals_ref.shape[0]
    chunk = min(CHUNK, slots)
    chunks = slots // chunk
    my_mem = lax.axis_index("mem")
    my_job = lax.axis_index("job")
    levels = mem_count // low
    level = my_mem // low
    place = my_mem % low

    barrier = pltpu.get_barrier_semaphore()

    def mem_peer(step):
        return partner(my_mem, mem_count - step, mem_count)

    def job_peer(step):
        return partner(my_job, job_count - step, job_count)

    def announce(mem):
        pl.semaphore_signal(barrier, inc=1, device_id=(mem, my_job), device_id_type=MESH)

    for distance in reversed(range(1, levels)):

        @pl.when(level + distance < levels)
        def _(distance=distance):
            for shift in range(low):
                announce((level + distance) * low + partner(place, shift, low))

    for shift in range(1, low):
        announce(level * low + partner(place, shift, low))

    @pl.when(level > 0)
    def _():
        announce(my_mem - low)

    for step in range(1, job_count):
        pl.semaphore_signal(
            barrier, inc=1, device_id=(my_mem, job_peer(step)), device_id_type=MESH
        )

    own_rows = pl.ds(pl.multiple_of(my_mem * jobs, jobs), jobs)
    small = [
        pltpu.make_async_copy(duals_ref, table.at[own_rows], small_sem.at[0]),
        pltpu.make_async_copy(owner_ref, owner_s, small_sem.at[1]),
        pltpu.make_async_copy(local_ref, local_s, small_sem.at[2]),
        pltpu.make_async_copy(member_ref, member_s, small_sem.at[3]),
        pltpu.make_async_copy(owner_ref, owner_v, small_sem.at[4]),
        pltpu.make_async_copy(local_ref, local_v, small_sem.at[5]),
        pltpu.make_async_copy(capacity_ref, capacity_v, small_sem.at[6]),
    ]
    for copy in small:
        copy.start()
    loads = []
    for part in range(chunks):
        rows = pl.ds(part * chunk, chunk)
        for index, (source, target) in enumerate(((cost_ref, cost_v), (coef_ref, coef_v))):
            copy = pltpu.make_async_copy(
                source.at[rows], target.at[rows], load_sem.at[2 * part + index]
            )
            copy.start()
            loads.append(copy)
    small[0].wait()

    above = jnp.where(level < levels - 1, 1, 0)
    pl.semaphore_wait(barrier, job_count - 1 + low - 1 + level * low + above)

    def push(rows, mem, send_sem, recv_sem):
        return pltpu.make_async_remote_copy(
            src_ref=table.at[rows],
            dst_ref=table.at[rows],
            send_sem=send_sem,
            recv_sem=recv_sem,
            device_id=(mem, my_job),
            device_id_type=MESH,
        )

    def beside(shift):
        mem = level * low + partner(place, shift, low)
        return push(own_rows, mem, beside_send.at[shift - 1], beside_recv.at[shift - 1])

    def down(distance, shift):
        mem = (level - distance) * low + partner(place, shift, low)
        index = (distance - 1) * low + shift
        return push(own_rows, mem, down_send.at[index], down_recv.at[index])

    def up(origin, shift):
        first = (origin * low + partner(place, shift, low)) * jobs
        rows = pl.ds(pl.multiple_of(first, jobs), jobs)
        index = origin * low + shift
        return push(rows, my_mem + low, up_send.at[index], up_recv.at[index])

    @pl.when(level < levels - 1)
    def _():
        for origin in range(levels - 1):

            @pl.when(level == origin)
            def _(origin=origin):
                up(origin, 0).start()

    for shift in range(1, low):
        beside(shift).start()
    for distance in reversed(range(1, levels)):

        @pl.when(level >= distance)
        def _(distance=distance):
            for shift in range(low):
                down(distance, shift).start()

    for origin in range(levels - 1):
        for shift in range(low):

            @pl.when(level > origin)
            def _(origin=origin, shift=shift):
                up(origin, shift).wait_recv()

            @pl.when((level > origin) & (level < levels - 1))
            def _(origin=origin, shift=shift):
                up(origin, shift).start()

        @pl.when(level == origin)
        def _(origin=origin):
            for shift in range(1, low):
                beside(shift).wait_recv()
                up(origin, shift).start()

    @pl.when(level == levels - 1)
    def _():
        for shift in range(1, low):
            beside(shift).wait_recv()

    for copy in small[1:]:
        copy.wait()
    for copy in loads:
        copy.wait()
    for distance in range(1, levels):

        @pl.when(level + distance < levels)
        def _(distance=distance):
            for shift in range(low):
                down(distance, shift).wait_recv()


    lanes = lax.broadcasted_iota(jnp.int32, (block, block), 1)
    members = jnp.zeros((block, block), jnp.float32)
    for part in range(chunks):

        def pair(index, members, part=part):
            halves = []
            marks = []
            for side in range(2):
                slot = part * chunk + 2 * index + side
                row = owner_s[0, slot] * jobs + local_s[0, slot]
                dual = -table[pl.ds(row, 1), :]
                coef = coef_v[slot].astype(jnp.float32)
                allocation = jnp.clip(
                    coef * dual - cost_v[slot].astype(jnp.float32), 0.0, 1.0
                )
                primal = allocation.astype(jnp.bfloat16)
                primal_ref[slot] = primal
                column[pl.ds(slot, 1), :] = jnp.sum(coef * allocation, axis=0, keepdims=True)
                halves.append(primal)
                marks.append((lanes == member_s[0, slot]).astype(jnp.float32).astype(jnp.bfloat16))
            return members + jnp.dot(
                jnp.concatenate(halves, axis=1),
                jnp.concatenate(marks, axis=0),
                preferred_element_type=jnp.float32,
            )

        members = lax.fori_loop(0, chunk // 2, pair, members, unroll=2)

    named = owner_v[...] * jobs + local_v[...]
    match = lax.broadcasted_iota(jnp.int32, (mem_count * jobs, slots), 0) == named
    match = match.astype(jnp.float32).astype(jnp.bfloat16)
    sums = column[...]
    high = sums.astype(jnp.bfloat16)
    rest = (sums - high.astype(jnp.float32)).astype(jnp.bfloat16)
    totals[...] = jnp.dot(match, high, preferred_element_type=jnp.float32) + jnp.dot(
        match, rest, preferred_element_type=jnp.float32
    )
    member_part[...] = members.T[:MB_DEV]

    sends = []
    for step in range(1, mem_count):
        peer = mem_peer(step)
        copy = pltpu.make_async_remote_copy(
            src_ref=totals.at[pl.ds(pl.multiple_of(peer * jobs, jobs), jobs)],
            dst_ref=incoming.at[step - 1],
            send_sem=column_send.at[step - 1],
            recv_sem=column_recv.at[step - 1],
            device_id=(peer, my_job),
            device_id_type=MESH,
        )
        copy.start()
        sends.append(copy)
    shares = []
    for step in range(1, job_count):
        copy = pltpu.make_async_remote_copy(
            src_ref=member_part,
            dst_ref=member_in.at[step - 1],
            send_sem=member_send.at[step - 1],
            recv_sem=member_recv.at[step - 1],
            device_id=(my_mem, job_peer(step)),
            device_id_type=MESH,
        )
        copy.start()
        shares.append(copy)

    share = member_part[...]
    for step, copy in enumerate(shares):
        copy.wait_recv()
        share = share + member_in[step]
    share_ref[...] = share * (1.0 / block)

    gradient = totals[own_rows, :] - capacity_v[...].astype(jnp.float32)
    for step, copy in enumerate(sends):
        copy.wait_recv()
        gradient = gradient + incoming[step]
    gradient_ref[...] = gradient

    for copy in sends + shares:
        copy.wait_send()
    for shift in range(1, low):
        beside(shift).wait_send()
    for distance in range(1, levels):

        @pl.when(level >= distance)
        def _(distance=distance):
            for shift in range(low):
                down(distance, shift).wait_send()

    for origin in range(levels - 1):

        @pl.when((level >= origin) & (level < levels - 1))
        def _(origin=origin):
            for shift in range(low):
                up(origin, shift).wait_send()


def solution(mesh):
    mem_count, job_count = mesh.shape["mem"], mesh.shape["job"]
    low = 2 if mem_count <= LEVELS * 2 else mem_count
    row = P(("mem", "job"))

    def per_device(pair_cost, pair_coef, slot_member, slot_owner, slot_local, duals, capacity):
        slots, block, _ = pair_cost.shape
        jobs = duals.shape[0]
        chunks = slots // min(CHUNK, slots)
        hbm = pl.BlockSpec(memory_space=pltpu.HBM)
        vmem = pl.BlockSpec(memory_space=pltpu.VMEM)
        dma = pltpu.SemaphoreType.DMA
        out_shape = (
            jax.ShapeDtypeStruct(pair_cost.shape, jnp.bfloat16),
            jax.ShapeDtypeStruct((jobs, block), jnp.float32),
            jax.ShapeDtypeStruct((MB_DEV, block), jnp.float32),
        )
        operands = (
            pair_cost,
            pair_coef,
            slot_member,
            slot_owner.reshape(1, slots),
            slot_local,
            duals,
            capacity,
        )
        operands = [pltpu.with_memory_space_constraint(value, pltpu.HBM) for value in operands]
        results = pl.pallas_call(
            functools.partial(kernel, mem_count, job_count, low),
            out_shape=out_shape,
            in_specs=[hbm] * 7,
            out_specs=(vmem,) * 3,
            scratch_shapes=[
                pltpu.VMEM(pair_cost.shape, jnp.bfloat16),
                pltpu.VMEM(pair_cost.shape, jnp.bfloat16),
                pltpu.SMEM((1, slots), jnp.int32),
                pltpu.SMEM((1, slots), jnp.int32),
                pltpu.SMEM((1, slots), jnp.int32),
                pltpu.VMEM((1, slots), jnp.int32),
                pltpu.VMEM((1, slots), jnp.int32),
                pltpu.VMEM((jobs, block), jnp.int32),
                pltpu.VMEM((mem_count * jobs, block), jnp.float32),
                pltpu.VMEM((slots, block), jnp.float32),
                pltpu.VMEM((mem_count * jobs, block), jnp.float32),
                pltpu.VMEM((mem_count - 1, jobs, block), jnp.float32),
                pltpu.VMEM((MB_DEV, block), jnp.float32),
                pltpu.VMEM((job_count - 1, MB_DEV, block), jnp.float32),
                dma((2 * chunks,)),
                dma((7,)),
                dma((max(low - 1, 1),)),
                dma((max(low - 1, 1),)),
                dma((mem_count,)),
                dma((mem_count,)),
                dma((mem_count,)),
                dma((mem_count,)),
                dma((mem_count - 1,)),
                dma((mem_count - 1,)),
                dma((job_count - 1,)),
                dma((job_count - 1,)),
            ],
            compiler_params=pltpu.CompilerParams(collective_id=0, has_side_effects=True, vmem_limit_bytes=VMEM_LIMIT),
)(*operands)
        return pl.pallas_call(
            finish,
            out_shape=out_shape,
            in_specs=[pl.BlockSpec(memory_space=pl.ANY)] * 3,
            out_specs=(hbm,) * 3,
            scratch_shapes=[dma((3,))],
            compiler_params=pltpu.CompilerParams(vmem_limit_bytes=VMEM_LIMIT),
        )(*results)

    return jax.shard_map(
        per_device,
        mesh=mesh,
        in_specs=(row,) * 7,
        out_specs=(row, row, P("mem")),
        check_vma=False,
    )
```

```python
import functools

import jax
import jax.numpy as jnp
from jax import lax
from jax.experimental import pallas as pl
from jax.experimental.pallas import tpu as pltpu
from jax.sharding import PartitionSpec as P

MB_DEV = 32
CHUNK = 8
GROUP = 8
VMEM_LIMIT = 16 << 20

MESH = pl.DeviceIdType.MESH


def partner(index, distance, count):
    assert count & (count - 1) == 0
    bit = 1
    while bit < count:
        if distance & bit:
            index = index + bit - 2 * bit * ((index // bit) % 2)
        bit *= 2
    return index


def finish(primal_in, gradient_in, share_in, primal_ref, gradient_ref, share_ref, sem):
    copies = [
        pltpu.make_async_copy(gradient_in, gradient_ref, sem.at[0]),
        pltpu.make_async_copy(share_in, share_ref, sem.at[1]),
    ]
    slots = primal_in.shape[0]
    chunk = min(CHUNK, slots)
    for part in range(slots // chunk):
        rows = pl.ds(part * chunk, chunk)
        copies.append(
            pltpu.make_async_copy(primal_in.at[rows], primal_ref.at[rows], sem.at[2 + part])
        )
    for copy in copies:
        copy.start()
    for copy in copies:
        copy.wait()


def kernel(
    mem_count,
    job_count,
    cost_ref,
    coef_ref,
    member_ref,
    owner_ref,
    local_ref,
    duals_ref,
    capacity_ref,
    primal_ref,
    gradient_ref,
    share_ref,
    cost_v,
    coef_v,
    member_s,
    owner_s,
    local_s,
    owner_v,
    local_v,
    capacity_v,
    table,
    column,
    totals,
    incoming,
    member_part,
    member_in,
    load_sem,
    small_sem,
    gather_send,
    gather_recv,
    column_send,
    column_recv,
    member_send,
    member_recv,
):
    slots, block = cost_v.shape[0], cost_v.shape[1]
    jobs = duals_ref.shape[0]
    chunk = min(CHUNK, slots)
    chunks = slots // chunk
    my_mem = lax.axis_index("mem")
    my_job = lax.axis_index("job")

    barrier = pltpu.get_barrier_semaphore()

    def mem_peer(step):
        return partner(my_mem, mem_count - step, mem_count)

    def job_peer(step):
        return partner(my_job, job_count - step, job_count)

    for step in range(1, mem_count):
        pl.semaphore_signal(
            barrier, inc=1, device_id=(mem_peer(step), my_job), device_id_type=MESH
        )
    for step in range(1, job_count):
        pl.semaphore_signal(
            barrier, inc=1, device_id=(my_mem, job_peer(step)), device_id_type=MESH
        )

    own_rows = pl.ds(pl.multiple_of(my_mem * jobs, jobs), jobs)
    small = [
        pltpu.make_async_copy(duals_ref, table.at[own_rows], small_sem.at[0]),
        pltpu.make_async_copy(owner_ref, owner_s, small_sem.at[1]),
        pltpu.make_async_copy(local_ref, local_s, small_sem.at[2]),
        pltpu.make_async_copy(member_ref, member_s, small_sem.at[3]),
        pltpu.make_async_copy(owner_ref, owner_v, small_sem.at[4]),
        pltpu.make_async_copy(local_ref, local_v, small_sem.at[5]),
        pltpu.make_async_copy(capacity_ref, capacity_v, small_sem.at[6]),
    ]
    for copy in small:
        copy.start()
    loads = []
    for part in range(chunks):
        rows = pl.ds(part * chunk, chunk)
        for index, (source, target) in enumerate(((cost_ref, cost_v), (coef_ref, coef_v))):
            copy = pltpu.make_async_copy(
                source.at[rows], target.at[rows], load_sem.at[2 * part + index]
            )
            copy.start()
            loads.append(copy)
    small[0].wait()

    pl.semaphore_wait(barrier, mem_count + job_count - 2)

    gathers = []
    for step in range(1, mem_count):
        copy = pltpu.make_async_remote_copy(
            src_ref=table.at[own_rows],
            dst_ref=table.at[own_rows],
            send_sem=gather_send.at[step - 1],
            recv_sem=gather_recv.at[step - 1],
            device_id=(mem_peer(step), my_job),
            device_id_type=MESH,
        )
        copy.start()
        gathers.append(copy)
    for copy in small[1:]:
        copy.wait()
    for copy in loads:
        copy.wait()
    for copy in gathers:
        copy.wait_recv()

    lanes = lax.broadcasted_iota(jnp.int32, (block, block), 1)
    members = jnp.zeros((block, block), jnp.float32)
    def group(index, members):
        parts = []
        marks = []
        for side in range(GROUP):
            slot = GROUP * index + side
            row = owner_s[0, slot] * jobs + local_s[0, slot]
            dual = -table[pl.ds(row, 1), :]
            coef = coef_v[slot].astype(jnp.float32)
            allocation = jnp.clip(coef * dual - cost_v[slot].astype(jnp.float32), 0.0, 1.0)
            primal = allocation.astype(jnp.bfloat16)
            primal_ref[slot] = primal
            column[pl.ds(slot, 1), :] = jnp.sum(coef * allocation, axis=0, keepdims=True)
            parts.append(primal)
            marks.append((lanes == member_s[0, slot]).astype(jnp.float32).astype(jnp.bfloat16))
        return members + jnp.dot(
            jnp.concatenate(parts, axis=1),
            jnp.concatenate(marks, axis=0),
            preferred_element_type=jnp.float32,
        )

    members = lax.fori_loop(0, slots // GROUP, group, members)

    named = owner_v[...] * jobs + local_v[...]
    match = lax.broadcasted_iota(jnp.int32, (mem_count * jobs, slots), 0) == named
    match = match.astype(jnp.float32).astype(jnp.bfloat16)
    sums = column[...]
    high = sums.astype(jnp.bfloat16)
    low = (sums - high.astype(jnp.float32)).astype(jnp.bfloat16)
    totals[...] = jnp.dot(match, high, preferred_element_type=jnp.float32) + jnp.dot(
        match, low, preferred_element_type=jnp.float32
    )
    member_part[...] = members.T[:MB_DEV]

    sends = []
    for step in range(1, mem_count):
        peer = mem_peer(step)
        copy = pltpu.make_async_remote_copy(
            src_ref=totals.at[pl.ds(pl.multiple_of(peer * jobs, jobs), jobs)],
            dst_ref=incoming.at[step - 1],
            send_sem=column_send.at[step - 1],
            recv_sem=column_recv.at[step - 1],
            device_id=(peer, my_job),
            device_id_type=MESH,
        )
        copy.start()
        sends.append(copy)
    shares = []
    for step in range(1, job_count):
        copy = pltpu.make_async_remote_copy(
            src_ref=member_part,
            dst_ref=member_in.at[step - 1],
            send_sem=member_send.at[step - 1],
            recv_sem=member_recv.at[step - 1],
            device_id=(my_mem, job_peer(step)),
            device_id_type=MESH,
        )
        copy.start()
        shares.append(copy)

    share = member_part[...]
    for step, copy in enumerate(shares):
        copy.wait_recv()
        share = share + member_in[step]
    share_ref[...] = share * (1.0 / block)

    gradient = totals[own_rows, :] - capacity_v[...].astype(jnp.float32)
    for step, copy in enumerate(sends):
        copy.wait_recv()
        gradient = gradient + incoming[step]
    gradient_ref[...] = gradient

    for copy in gathers + sends + shares:
        copy.wait_send()


def solution(mesh):
    mem_count, job_count = mesh.shape["mem"], mesh.shape["job"]
    row = P(("mem", "job"))

    def per_device(pair_cost, pair_coef, slot_member, slot_owner, slot_local, duals, capacity):
        slots, block, _ = pair_cost.shape
        jobs = duals.shape[0]
        chunks = slots // min(CHUNK, slots)
        hbm = pl.BlockSpec(memory_space=pltpu.HBM)
        vmem = pl.BlockSpec(memory_space=pltpu.VMEM)
        dma = pltpu.SemaphoreType.DMA
        out_shape = (
            jax.ShapeDtypeStruct(pair_cost.shape, jnp.bfloat16),
            jax.ShapeDtypeStruct((jobs, block), jnp.float32),
            jax.ShapeDtypeStruct((MB_DEV, block), jnp.float32),
        )
        operands = (
            pair_cost,
            pair_coef,
            slot_member,
            slot_owner.reshape(1, slots),
            slot_local,
            duals,
            capacity,
        )
        operands = [pltpu.with_memory_space_constraint(value, pltpu.HBM) for value in operands]
        results = pl.pallas_call(
            functools.partial(kernel, mem_count, job_count),
            out_shape=out_shape,
            in_specs=[hbm] * 7,
            out_specs=(vmem,) * 3,
            scratch_shapes=[
                pltpu.VMEM(pair_cost.shape, jnp.bfloat16),
                pltpu.VMEM(pair_cost.shape, jnp.bfloat16),
                pltpu.SMEM((1, slots), jnp.int32),
                pltpu.SMEM((1, slots), jnp.int32),
                pltpu.SMEM((1, slots), jnp.int32),
                pltpu.VMEM((1, slots), jnp.int32),
                pltpu.VMEM((1, slots), jnp.int32),
                pltpu.VMEM((jobs, block), jnp.int32),
                pltpu.VMEM((mem_count * jobs, block), jnp.float32),
                pltpu.VMEM((slots, block), jnp.float32),
                pltpu.VMEM((mem_count * jobs, block), jnp.float32),
                pltpu.VMEM((mem_count - 1, jobs, block), jnp.float32),
                pltpu.VMEM((MB_DEV, block), jnp.float32),
                pltpu.VMEM((job_count - 1, MB_DEV, block), jnp.float32),
                dma((2 * chunks,)),
                dma((7,)),
                dma((mem_count - 1,)),
                dma((mem_count - 1,)),
                dma((mem_count - 1,)),
                dma((mem_count - 1,)),
                dma((job_count - 1,)),
                dma((job_count - 1,)),
            ],
            compiler_params=pltpu.CompilerParams(
                collective_id=0, has_side_effects=True, vmem_limit_bytes=VMEM_LIMIT
            ),
        )(*operands)
        return pl.pallas_call(
            finish,
            out_shape=out_shape,
            in_specs=[pl.BlockSpec(memory_space=pl.ANY)] * 3,
            out_specs=(hbm,) * 3,
            scratch_shapes=[dma((2 + chunks,))],
            compiler_params=pltpu.CompilerParams(vmem_limit_bytes=VMEM_LIMIT),
        )(*results)

    return jax.shard_map(
        per_device,
        mesh=mesh,
        in_specs=(row,) * 7,
        out_specs=(row, row, P("mem")),
        check_vma=False,
    )
```

```python
import functools

import jax
import jax.numpy as jnp
from jax import lax
from jax.experimental import pallas as pl
from jax.experimental.pallas import tpu as pltpu
from jax.sharding import PartitionSpec as P

MB_DEV = 32
CHUNK = 8
GROUP = 8
VMEM_LIMIT = 16 << 20

MESH = pl.DeviceIdType.MESH


def partner(index, distance, count):
    assert count & (count - 1) == 0
    bit = 1
    while bit < count:
        if distance & bit:
            index = index + bit - 2 * bit * ((index // bit) % 2)
        bit *= 2
    return index


def finish(primal_in, gradient_in, share_in, primal_ref, gradient_ref, share_ref, sem):
    copies = [
        pltpu.make_async_copy(gradient_in, gradient_ref, sem.at[0]),
        pltpu.make_async_copy(share_in, share_ref, sem.at[1]),
    ]
    slots = primal_in.shape[0]
    chunk = min(CHUNK, slots)
    for part in range(slots // chunk):
        rows = pl.ds(part * chunk, chunk)
        copies.append(
            pltpu.make_async_copy(primal_in.at[rows], primal_ref.at[rows], sem.at[2 + part])
        )
    for copy in copies:
        copy.start()
    for copy in copies:
        copy.wait()


def kernel(
    mem_count,
    job_count,
    cost_ref,
    coef_ref,
    member_ref,
    owner_ref,
    local_ref,
    duals_ref,
    capacity_ref,
    primal_ref,
    gradient_ref,
    share_ref,
    cost_v,
    coef_v,
    member_s,
    owner_s,
    local_s,
    owner_v,
    local_v,
    capacity_v,
    table,
    column,
    totals,
    incoming,
    member_part,
    member_in,
    load_sem,
    small_sem,
    gather_send,
    gather_recv,
    column_send,
    column_recv,
    member_send,
    member_recv,
):
    slots, block = cost_v.shape[0], cost_v.shape[1]
    jobs = duals_ref.shape[0]
    chunk = min(CHUNK, slots)
    chunks = slots // chunk
    my_mem = lax.axis_index("mem")
    my_job = lax.axis_index("job")

    barrier = pltpu.get_barrier_semaphore()

    def mem_peer(step):
        return partner(my_mem, mem_count - step, mem_count)

    def job_peer(step):
        return partner(my_job, job_count - step, job_count)

    for step in range(1, mem_count):
        pl.semaphore_signal(
            barrier, inc=1, device_id=(mem_peer(step), my_job), device_id_type=MESH
        )
    for step in range(1, job_count):
        pl.semaphore_signal(
            barrier, inc=1, device_id=(my_mem, job_peer(step)), device_id_type=MESH
        )

    own_rows = pl.ds(pl.multiple_of(my_mem * jobs, jobs), jobs)
    small = [
        pltpu.make_async_copy(duals_ref, table.at[own_rows], small_sem.at[0]),
        pltpu.make_async_copy(owner_ref, owner_s, small_sem.at[1]),
        pltpu.make_async_copy(local_ref, local_s, small_sem.at[2]),
        pltpu.make_async_copy(member_ref, member_s, small_sem.at[3]),
        pltpu.make_async_copy(owner_ref, owner_v, small_sem.at[4]),
        pltpu.make_async_copy(local_ref, local_v, small_sem.at[5]),
        pltpu.make_async_copy(capacity_ref, capacity_v, small_sem.at[6]),
    ]
    for copy in small:
        copy.start()
    loads = []
    for part in range(chunks):
        rows = pl.ds(part * chunk, chunk)
        for index, (source, target) in enumerate(((cost_ref, cost_v), (coef_ref, coef_v))):
            copy = pltpu.make_async_copy(
                source.at[rows], target.at[rows], load_sem.at[2 * part + index]
            )
            copy.start()
            loads.append(copy)
    small[0].wait()

    pl.semaphore_wait(barrier, mem_count + job_count - 2)

    gathers = []
    for step in range(1, mem_count):
        copy = pltpu.make_async_remote_copy(
            src_ref=table.at[own_rows],
            dst_ref=table.at[own_rows],
            send_sem=gather_send.at[step - 1],
            recv_sem=gather_recv.at[step - 1],
            device_id=(mem_peer(step), my_job),
            device_id_type=MESH,
        )
        copy.start()
        gathers.append(copy)
    for copy in small[1:]:
        copy.wait()
    for copy in loads:
        copy.wait()
    for copy in gathers:
        copy.wait_recv()

    def allocate(index, carry):
        for side in range(GROUP):
            slot = GROUP * index + side
            row = owner_s[0, slot] * jobs + local_s[0, slot]
            dual = -table[pl.ds(row, 1), :]
            coef = coef_v[slot].astype(jnp.float32)
            allocation = jnp.clip(coef * dual - cost_v[slot].astype(jnp.float32), 0.0, 1.0)
            primal_ref[slot] = allocation.astype(jnp.bfloat16)
            column[pl.ds(slot, 1), :] = jnp.sum(coef * allocation, axis=0, keepdims=True)
        return carry

    lax.fori_loop(0, slots // GROUP, allocate, 0)

    named = owner_v[...] * jobs + local_v[...]
    match = lax.broadcasted_iota(jnp.int32, (mem_count * jobs, slots), 0) == named
    match = match.astype(jnp.float32).astype(jnp.bfloat16)
    sums = column[...]
    high = sums.astype(jnp.bfloat16)
    low = (sums - high.astype(jnp.float32)).astype(jnp.bfloat16)
    totals[...] = jnp.dot(match, high, preferred_element_type=jnp.float32) + jnp.dot(
        match, low, preferred_element_type=jnp.float32
    )

    sends = []
    for step in range(1, mem_count):
        peer = mem_peer(step)
        copy = pltpu.make_async_remote_copy(
            src_ref=totals.at[pl.ds(pl.multiple_of(peer * jobs, jobs), jobs)],
            dst_ref=incoming.at[step - 1],
            send_sem=column_send.at[step - 1],
            recv_sem=column_recv.at[step - 1],
            device_id=(peer, my_job),
            device_id_type=MESH,
        )
        copy.start()
        sends.append(copy)
    lanes = lax.broadcasted_iota(jnp.int32, (block, block), 1)

    def group(index, members):
        first = GROUP * index
        parts = [primal_ref[first + side] for side in range(GROUP)]
        marks = [
            (lanes == member_s[0, first + side]).astype(jnp.float32).astype(jnp.bfloat16)
            for side in range(GROUP)
        ]
        return members + jnp.dot(
            jnp.concatenate(parts, axis=1),
            jnp.concatenate(marks, axis=0),
            preferred_element_type=jnp.float32,
        )

    members = lax.fori_loop(
        0, slots // GROUP, group, jnp.zeros((block, block), jnp.float32)
    )
    member_part[...] = members.T[:MB_DEV]
    shares = []
    for step in range(1, job_count):
        copy = pltpu.make_async_remote_copy(
            src_ref=member_part,
            dst_ref=member_in.at[step - 1],
            send_sem=member_send.at[step - 1],
            recv_sem=member_recv.at[step - 1],
            device_id=(my_mem, job_peer(step)),
            device_id_type=MESH,
        )
        copy.start()
        shares.append(copy)

    share = member_part[...]
    for step, copy in enumerate(shares):
        copy.wait_recv()
        share = share + member_in[step]
    share_ref[...] = share * (1.0 / block)

    gradient = totals[own_rows, :] - capacity_v[...].astype(jnp.float32)
    for step, copy in enumerate(sends):
        copy.wait_recv()
        gradient = gradient + incoming[step]
    gradient_ref[...] = gradient

    for copy in gathers + sends + shares:
        copy.wait_send()


def solution(mesh):
    mem_count, job_count = mesh.shape["mem"], mesh.shape["job"]
    row = P(("mem", "job"))

    def per_device(pair_cost, pair_coef, slot_member, slot_owner, slot_local, duals, capacity):
        slots, block, _ = pair_cost.shape
        jobs = duals.shape[0]
        chunks = slots // min(CHUNK, slots)
        hbm = pl.BlockSpec(memory_space=pltpu.HBM)
        vmem = pl.BlockSpec(memory_space=pltpu.VMEM)
        dma = pltpu.SemaphoreType.DMA
        out_shape = (
            jax.ShapeDtypeStruct(pair_cost.shape, jnp.bfloat16),
            jax.ShapeDtypeStruct((jobs, block), jnp.float32),
            jax.ShapeDtypeStruct((MB_DEV, block), jnp.float32),
        )
        operands = (
            pair_cost,
            pair_coef,
            slot_member,
            slot_owner.reshape(1, slots),
            slot_local,
            duals,
            capacity,
        )
        operands = [pltpu.with_memory_space_constraint(value, pltpu.HBM) for value in operands]
        results = pl.pallas_call(
            functools.partial(kernel, mem_count, job_count),
            out_shape=out_shape,
            in_specs=[hbm] * 7,
            out_specs=(vmem,) * 3,
            scratch_shapes=[
                pltpu.VMEM(pair_cost.shape, jnp.bfloat16),
                pltpu.VMEM(pair_cost.shape, jnp.bfloat16),
                pltpu.SMEM((1, slots), jnp.int32),
                pltpu.SMEM((1, slots), jnp.int32),
                pltpu.SMEM((1, slots), jnp.int32),
                pltpu.VMEM((1, slots), jnp.int32),
                pltpu.VMEM((1, slots), jnp.int32),
                pltpu.VMEM((jobs, block), jnp.int32),
                pltpu.VMEM((mem_count * jobs, block), jnp.float32),
                pltpu.VMEM((slots, block), jnp.float32),
                pltpu.VMEM((mem_count * jobs, block), jnp.float32),
                pltpu.VMEM((mem_count - 1, jobs, block), jnp.float32),
                pltpu.VMEM((MB_DEV, block), jnp.float32),
                pltpu.VMEM((job_count - 1, MB_DEV, block), jnp.float32),
                dma((2 * chunks,)),
                dma((7,)),
                dma((mem_count - 1,)),
                dma((mem_count - 1,)),
                dma((mem_count - 1,)),
                dma((mem_count - 1,)),
                dma((job_count - 1,)),
                dma((job_count - 1,)),
            ],
            compiler_params=pltpu.CompilerParams(
                collective_id=0, has_side_effects=True, vmem_limit_bytes=VMEM_LIMIT
            ),
        )(*operands)
        return pl.pallas_call(
            finish,
            out_shape=out_shape,
            in_specs=[pl.BlockSpec(memory_space=pl.ANY)] * 3,
            out_specs=(hbm,) * 3,
            scratch_shapes=[dma((2 + chunks,))],
            compiler_params=pltpu.CompilerParams(vmem_limit_bytes=VMEM_LIMIT),
        )(*results)

    return jax.shard_map(
        per_device,
        mesh=mesh,
        in_specs=(row,) * 7,
        out_specs=(row, row, P("mem")),
        check_vma=False,
    )
```

```python
import functools

import jax
import jax.numpy as jnp
from jax import lax
from jax.experimental import pallas as pl
from jax.experimental.pallas import tpu as pltpu
from jax.sharding import PartitionSpec as P

MB_DEV = 32
CHUNK = 8
GROUP = 8
VMEM_LIMIT = 16 << 20

MESH = pl.DeviceIdType.MESH


def partner(index, distance, count):
    assert count & (count - 1) == 0
    bit = 1
    while bit < count:
        if distance & bit:
            index = index + bit - 2 * bit * ((index // bit) % 2)
        bit *= 2
    return index


def finish(primal_in, gradient_in, share_in, primal_ref, gradient_ref, share_ref, sem):
    copies = [
        pltpu.make_async_copy(gradient_in, gradient_ref, sem.at[0]),
        pltpu.make_async_copy(share_in, share_ref, sem.at[1]),
    ]
    slots = primal_in.shape[0]
    chunk = min(CHUNK, slots)
    for part in range(slots // chunk):
        rows = pl.ds(part * chunk, chunk)
        copies.append(
            pltpu.make_async_copy(primal_in.at[rows], primal_ref.at[rows], sem.at[2 + part])
        )
    for copy in copies:
        copy.start()
    for copy in copies:
        copy.wait()


def kernel(
    mem_count,
    job_count,
    cost_ref,
    coef_ref,
    member_ref,
    owner_ref,
    local_ref,
    duals_ref,
    capacity_ref,
    primal_ref,
    gradient_ref,
    share_ref,
    cost_v,
    coef_v,
    member_s,
    owner_s,
    local_s,
    owner_v,
    local_v,
    capacity_v,
    table,
    column,
    totals,
    incoming,
    member_part,
    member_in,
    load_sem,
    small_sem,
    gather_send,
    gather_recv,
    column_send,
    column_recv,
    member_send,
    member_recv,
):
    slots, block = cost_v.shape[0], cost_v.shape[1]
    jobs = duals_ref.shape[0]
    chunk = min(CHUNK, slots)
    chunks = slots // chunk
    my_mem = lax.axis_index("mem")
    my_job = lax.axis_index("job")

    barrier = pltpu.get_barrier_semaphore()

    def mem_peer(step):
        return partner(my_mem, mem_count - step, mem_count)

    def job_peer(step):
        return partner(my_job, job_count - step, job_count)

    for step in range(1, mem_count):
        pl.semaphore_signal(
            barrier, inc=1, device_id=(mem_peer(step), my_job), device_id_type=MESH
        )
    for step in range(1, job_count):
        pl.semaphore_signal(
            barrier, inc=1, device_id=(my_mem, job_peer(step)), device_id_type=MESH
        )

    own_rows = pl.ds(pl.multiple_of(my_mem * jobs, jobs), jobs)
    small = [
        pltpu.make_async_copy(duals_ref, table.at[own_rows], small_sem.at[0]),
        pltpu.make_async_copy(owner_ref, owner_s, small_sem.at[1]),
        pltpu.make_async_copy(local_ref, local_s, small_sem.at[2]),
        pltpu.make_async_copy(member_ref, member_s, small_sem.at[3]),
        pltpu.make_async_copy(owner_ref, owner_v, small_sem.at[4]),
        pltpu.make_async_copy(local_ref, local_v, small_sem.at[5]),
        pltpu.make_async_copy(capacity_ref, capacity_v, small_sem.at[6]),
    ]
    for copy in small:
        copy.start()
    loads = []
    for part in range(chunks):
        rows = pl.ds(part * chunk, chunk)
        for index, (source, target) in enumerate(((cost_ref, cost_v), (coef_ref, coef_v))):
            copy = pltpu.make_async_copy(
                source.at[rows], target.at[rows], load_sem.at[2 * part + index]
            )
            copy.start()
            loads.append(copy)
    small[0].wait()

    pl.semaphore_wait(barrier, mem_count + job_count - 2)

    def gather(peer, index):
        return pltpu.make_async_remote_copy(
            src_ref=table.at[own_rows],
            dst_ref=table.at[own_rows],
            send_sem=gather_send.at[index],
            recv_sem=gather_recv.at[index],
            device_id=(peer, my_job),
            device_id_type=MESH,
        )

    def index_of(target):
        return mem_count - 1 - partner(my_mem, target, mem_count)

    gathers = [gather(mem_peer(step), step - 1) for step in range(1, mem_count)]
    for target in reversed(range(mem_count)):

        @pl.when(my_mem != target)
        def _(target=target):
            gather(target, index_of(target)).start()

    for copy in small[1:]:
        copy.wait()
    for copy in loads:
        copy.wait()
    for copy in gathers:
        copy.wait_recv()

    def allocate(index, carry):
        for side in range(GROUP):
            slot = GROUP * index + side
            row = owner_s[0, slot] * jobs + local_s[0, slot]
            dual = -table[pl.ds(row, 1), :]
            coef = coef_v[slot].astype(jnp.float32)
            allocation = jnp.clip(coef * dual - cost_v[slot].astype(jnp.float32), 0.0, 1.0)
            primal_ref[slot] = allocation.astype(jnp.bfloat16)
            column[pl.ds(slot, 1), :] = jnp.sum(coef * allocation, axis=0, keepdims=True)
        return carry

    lax.fori_loop(0, slots // GROUP, allocate, 0)

    named = owner_v[...] * jobs + local_v[...]
    match = lax.broadcasted_iota(jnp.int32, (mem_count * jobs, slots), 0) == named
    match = match.astype(jnp.float32).astype(jnp.bfloat16)
    sums = column[...]
    high = sums.astype(jnp.bfloat16)
    low = (sums - high.astype(jnp.float32)).astype(jnp.bfloat16)
    totals[...] = jnp.dot(match, high, preferred_element_type=jnp.float32) + jnp.dot(
        match, low, preferred_element_type=jnp.float32
    )

    def send(peer, index):
        return pltpu.make_async_remote_copy(
            src_ref=totals.at[pl.ds(pl.multiple_of(peer * jobs, jobs), jobs)],
            dst_ref=incoming.at[index],
            send_sem=column_send.at[index],
            recv_sem=column_recv.at[index],
            device_id=(peer, my_job),
            device_id_type=MESH,
        )

    sends = [send(mem_peer(step), step - 1) for step in range(1, mem_count)]
    for target in range(mem_count):

        @pl.when(my_mem != target)
        def _(target=target):
            send(target, index_of(target)).start()

    lanes = lax.broadcasted_iota(jnp.int32, (block, block), 1)

    def group(index, members):
        first = GROUP * index
        parts = [primal_ref[first + side] for side in range(GROUP)]
        marks = [
            (lanes == member_s[0, first + side]).astype(jnp.float32).astype(jnp.bfloat16)
            for side in range(GROUP)
        ]
        return members + jnp.dot(
            jnp.concatenate(parts, axis=1),
            jnp.concatenate(marks, axis=0),
            preferred_element_type=jnp.float32,
        )

    members = lax.fori_loop(
        0, slots // GROUP, group, jnp.zeros((block, block), jnp.float32)
    )
    member_part[...] = members.T[:MB_DEV]
    shares = []
    for step in range(1, job_count):
        copy = pltpu.make_async_remote_copy(
            src_ref=member_part,
            dst_ref=member_in.at[step - 1],
            send_sem=member_send.at[step - 1],
            recv_sem=member_recv.at[step - 1],
            device_id=(my_mem, job_peer(step)),
            device_id_type=MESH,
        )
        copy.start()
        shares.append(copy)

    share = member_part[...]
    for step, copy in enumerate(shares):
        copy.wait_recv()
        share = share + member_in[step]
    share_ref[...] = share * (1.0 / block)

    gradient = totals[own_rows, :] - capacity_v[...].astype(jnp.float32)
    for step, copy in enumerate(sends):
        copy.wait_recv()
        gradient = gradient + incoming[step]
    gradient_ref[...] = gradient

    for copy in gathers + sends + shares:
        copy.wait_send()


def solution(mesh):
    mem_count, job_count = mesh.shape["mem"], mesh.shape["job"]
    row = P(("mem", "job"))

    def per_device(pair_cost, pair_coef, slot_member, slot_owner, slot_local, duals, capacity):
        slots, block, _ = pair_cost.shape
        jobs = duals.shape[0]
        chunks = slots // min(CHUNK, slots)
        hbm = pl.BlockSpec(memory_space=pltpu.HBM)
        vmem = pl.BlockSpec(memory_space=pltpu.VMEM)
        dma = pltpu.SemaphoreType.DMA
        out_shape = (
            jax.ShapeDtypeStruct(pair_cost.shape, jnp.bfloat16),
            jax.ShapeDtypeStruct((jobs, block), jnp.float32),
            jax.ShapeDtypeStruct((MB_DEV, block), jnp.float32),
        )
        operands = (
            pair_cost,
            pair_coef,
            slot_member,
            slot_owner.reshape(1, slots),
            slot_local,
            duals,
            capacity,
        )
        operands = [pltpu.with_memory_space_constraint(value, pltpu.HBM) for value in operands]
        results = pl.pallas_call(
            functools.partial(kernel, mem_count, job_count),
            out_shape=out_shape,
            in_specs=[hbm] * 7,
            out_specs=(vmem,) * 3,
            scratch_shapes=[
                pltpu.VMEM(pair_cost.shape, jnp.bfloat16),
                pltpu.VMEM(pair_cost.shape, jnp.bfloat16),
                pltpu.SMEM((1, slots), jnp.int32),
                pltpu.SMEM((1, slots), jnp.int32),
                pltpu.SMEM((1, slots), jnp.int32),
                pltpu.VMEM((1, slots), jnp.int32),
                pltpu.VMEM((1, slots), jnp.int32),
                pltpu.VMEM((jobs, block), jnp.int32),
                pltpu.VMEM((mem_count * jobs, block), jnp.float32),
                pltpu.VMEM((slots, block), jnp.float32),
                pltpu.VMEM((mem_count * jobs, block), jnp.float32),
                pltpu.VMEM((mem_count - 1, jobs, block), jnp.float32),
                pltpu.VMEM((MB_DEV, block), jnp.float32),
                pltpu.VMEM((job_count - 1, MB_DEV, block), jnp.float32),
                dma((2 * chunks,)),
                dma((7,)),
                dma((mem_count - 1,)),
                dma((mem_count - 1,)),
                dma((mem_count - 1,)),
                dma((mem_count - 1,)),
                dma((job_count - 1,)),
                dma((job_count - 1,)),
            ],
            compiler_params=pltpu.CompilerParams(
                collective_id=0, has_side_effects=True, vmem_limit_bytes=VMEM_LIMIT
            ),
        )(*operands)
        return pl.pallas_call(
            finish,
            out_shape=out_shape,
            in_specs=[pl.BlockSpec(memory_space=pl.ANY)] * 3,
            out_specs=(hbm,) * 3,
            scratch_shapes=[dma((2 + chunks,))],
            compiler_params=pltpu.CompilerParams(vmem_limit_bytes=VMEM_LIMIT),
        )(*results)

    return jax.shard_map(
        per_device,
        mesh=mesh,
        in_specs=(row,) * 7,
        out_specs=(row, row, P("mem")),
        check_vma=False,
    )
```
